32 devices in a mesh: blk: 4 (over z), grp: 8 (over y, x, core).
Axes of the slice: x: 2, y: 2, z: 4, core: 2. Of those that a mesh axis runs over, the one named last changes fastest.
Arguments:
- position: float32 [3, 16384], P(None, ('blk', 'grp')), may hold values from -6 to 6
- velocity: float32 [3, 16384], P(None, ('blk', 'grp')), may hold values from -6 to 6
- accel_old: float32 [3, 16384], P(None, ('blk', 'grp')), may hold values from -6 to 6
- jerk_old: float32 [3, 16384], P(None, ('blk', 'grp')), may hold values from -6 to 6
- mass: float32 [16384], P(('blk', 'grp')), may hold values from 1e-07 to 1e-05
- elapsed: float32 [16384], P(('blk', 'grp')), may hold values from 0.1 to 1
- active_index: int32 [512], P(('blk', 'grp')), may hold values from 0 to 16383, as said below
Outputs:
- predicted: float32 [6, 16384], P(None, ('blk', 'grp'))
- accel: float32 [3, 512], P(None, ('blk', 'grp'))
- jerk: float32 [3, 512], P(None, ('blk', 'grp'))
The draws below stay inside these ranges and needn't reach their ends.
Inputs may be any that keep to these rules, and one draw needn't show every extreme that they name: `active_index`: entries 16 * k to 16 * k + 15 are distinct stars of the range 512 * k to 512 * k + 511, for every k.
All inputs are finite; a program needn't handle non-finite values.
Results may differ from the reference program's by a relative error of at most 0.0003.
Values sent between devices are 32-bit elements; how exact they have to be, the bound alone decides.
A program may use at most 64 MiB of HBM per device.

```python
import math
import jax
import jax.numpy as jnp
from jax import lax

STAR_DEV = 512
ACT_DEV = 16
N_STARS = 16384


def draw_active_index(key, part):
    shards = N_STARS // STAR_DEV
    subkeys = jax.random.split(key, shards)
    picked = jax.vmap(lambda single: jax.random.permutation(single, STAR_DEV)[:ACT_DEV])(subkeys)
    offset = jnp.arange(shards, dtype=jnp.int32)[:, None] * STAR_DEV
    return (picked.astype(jnp.int32) + offset).reshape(-1)


def block_scale(stream_key, extent, cuts, low, high):
    level, own = 1.0, jax.random.fold_in(stream_key, 6)
    for axis_at, blocks in cuts:
        heights = jnp.exp(jax.random.uniform(jax.random.fold_in(own, axis_at), (blocks,), jnp.float32, low / len(cuts), high / len(cuts)))
        level = level * jnp.repeat(heights, extent[axis_at] // blocks).reshape([-1 if axis == axis_at else 1 for axis in range(len(extent))])
    return level


def gaussian(key, shape, scale, bound, cuts=(), kind=jnp.bfloat16):
    loudness = block_scale(key, shape, cuts, -0.22, 0.18) if cuts else 1.0
    drawn = jax.random.normal(key, shape, jnp.float32) * scale * loudness
    return jnp.minimum(jnp.maximum(drawn, -bound), bound).astype(kind)


def setup_inputs(seed: int = 0) -> dict:
    splits = jax.random.split(jax.random.key(seed), 8)
    position = gaussian(splits[0], (3, N_STARS), 1.0, 6.0, ((1, 32),), jnp.float32)
    velocity = gaussian(splits[1], (3, N_STARS), 0.7, 6.0, ((1, 32),), jnp.float32)
    accel_old = gaussian(splits[2], (3, N_STARS), 1.0, 6.0, ((1, 32),), jnp.float32)
    jerk_old = gaussian(splits[3], (3, N_STARS), 1.0, 6.0, ((1, 32),), jnp.float32)
    mass = jnp.clip(jnp.exp(math.log(9.999999747378752e-06) - 4.6051701 * jax.random.uniform(splits[4], (N_STARS,), jnp.float32) ** block_scale(splits[4], (N_STARS,), ((0, 32),), -0.2, 0.2)), 1.0000000116860974e-07, 9.999999747378752e-06)
    elapsed = jnp.clip(jnp.exp(math.log(1.0) - 2.3025851 * jax.random.uniform(splits[5], (N_STARS,), jnp.float32) ** block_scale(splits[5], (N_STARS,), ((0, 32),), -0.2, 0.2)), 0.1, 1.0)
    active_index = draw_active_index(jax.random.fold_in(splits[7], 71), 0)
    return dict(position=position, velocity=velocity, accel_old=accel_old, jerk_old=jerk_old, mass=mass, elapsed=elapsed, active_index=active_index)


SOFTENING = 0.0001

def predict(position, velocity, accel_old, jerk_old, elapsed):
    step_row = elapsed[None, :]
    half = step_row * step_row * 0.5
    sixth = half * step_row * (1.0 / 3.0)
    new_position = position + step_row * velocity + half * accel_old + sixth * jerk_old
    new_velocity = velocity + step_row * accel_old + half * jerk_old
    return jnp.concatenate([new_position, new_velocity], 0)

def interact(targets, sources, masses, block_limit):
    columns = targets.shape[1]
    block_size = math.gcd(columns, block_limit)
    blocks = columns // block_size
    stacked = targets.reshape(6, blocks, block_size).transpose(1, 0, 2)

    def one_block(target_block):
        separation = sources[0:3][:, None, :] - target_block[0:3][:, :, None]
        relative = sources[3:6][:, None, :] - target_block[3:6][:, :, None]
        distance = lax.optimization_barrier(jnp.sum(separation * separation, 0)) + SOFTENING
        inverse = 1.0 / jnp.sqrt(distance)
        weight = masses[None, :] * inverse * inverse * inverse
        radial = 3.0 * lax.optimization_barrier(jnp.sum(separation * relative, 0)) / distance
        accel_part = lax.optimization_barrier(jnp.sum(weight[None] * separation, 2))
        jerk_part = lax.optimization_barrier(jnp.sum(weight[None] * (relative - radial[None] * separation), 2))
        return jnp.concatenate([accel_part, jerk_part], 0)
    result = lax.map(one_block, stacked)
    return result.transpose(1, 0, 2).reshape(6, columns)

def reference(position, velocity, accel_old, jerk_old, mass, elapsed, active_index):
    predicted = predict(position, velocity, accel_old, jerk_old, elapsed)
    targets = jnp.take(predicted, active_index, axis=1)
    shards = N_STARS // STAR_DEV
    source_blocks = predicted.reshape(6, shards, STAR_DEV).transpose(1, 0, 2)
    mass_blocks = mass.reshape(shards, STAR_DEV)

    def accumulate(total, pieces):
        return (total + interact(targets, pieces[0], pieces[1], 1024), None)
    start = jnp.zeros((6, targets.shape[1]), jnp.float32)
    totals, unused = lax.scan(accumulate, start, (source_blocks, mass_blocks))
    return (predicted, totals[0:3], totals[3:6])
```

```python
import functools

import jax
import jax.numpy as jnp
from jax import lax
from jax.experimental import pallas as pl
from jax.experimental.pallas import tpu as pltpu
from jax.sharding import PartitionSpec as P

SOFTENING = 0.0001
LANES = 128
ROWS = 8


def flipped(index, mask):
    out, bit = index, 1
    while bit <= mask:
        if mask & bit:
            out = out + bit - 2 * bit * lax.rem(lax.div(index, bit), 2)
        bit *= 2
    return out


def kernel(
    n_blk, n_grp, stars, active,
    position, velocity, accel_old, jerk_old, mass, elapsed, index,
    predicted, accel, jerk,
    in_pos, in_vel, in_acc, in_jrk, in_mass, in_time, in_index,
    out_pred, out_acc, out_jrk,
    sources, targets, spread, sums, parts, arrived,
    in_sem, out_sem, src_send, src_recv, tgt_send, tgt_recv, sum_send, sum_recv,
):
    blk, grp = lax.axis_index("blk"), lax.axis_index("grp")
    groups, chunks = active // ROWS, stars // LANES
    power_of_two = n_grp & (n_grp - 1) == 0

    def mate(k):
        return flipped(grp, k) if power_of_two else lax.rem(grp + k, n_grp)

    def back(k):
        return k if power_of_two else n_grp - k

    def ahead(k):
        return lax.rem(blk + k, n_blk)

    barrier = pltpu.get_barrier_semaphore()
    for k in range(1, n_blk):
        pl.semaphore_signal(barrier, inc=1, device_id={"blk": ahead(k)}, device_id_type=pl.DeviceIdType.MESH)
    for k in range(1, n_grp):
        pl.semaphore_signal(barrier, inc=1, device_id={"grp": mate(k)}, device_id_type=pl.DeviceIdType.MESH)

    loads = [
        pltpu.make_async_copy(whole, held, in_sem.at[at])
        for at, (whole, held) in enumerate((
            (position, in_pos), (velocity, in_vel), (accel_old, in_acc), (jerk_old, in_jrk),
            (mass, in_mass), (elapsed, in_time), (index, in_index),
        ))
    ]
    for load in loads:
        load.start()
    for load in loads:
        load.wait()

    step_row = in_time[...]
    half = step_row * step_row * 0.5
    sixth = half * step_row * (1.0 / 3.0)
    new_position = in_pos[...] + step_row * in_vel[...] + half * in_acc[...] + sixth * in_jrk[...]
    new_velocity = in_vel[...] + step_row * in_acc[...] + half * in_jrk[...]
    sources[0, 0:3, :] = new_position
    sources[0, 3:6, :] = new_velocity
    sources[0, 6:7, :] = in_mass[...]
    out_pred[0:3, :] = new_position
    out_pred[3:6, :] = new_velocity

    base = (blk * n_grp + grp) * stars
    offsets = (in_index[...] - base).astype(jnp.float32)
    lane_active = lax.broadcasted_iota(jnp.int32, (ROWS, active), 1)
    row_active = lax.broadcasted_iota(jnp.int32, (ROWS, active), 0)
    lane_stars = lax.broadcasted_iota(jnp.int32, (ROWS, stars), 1)
    lane = lax.broadcasted_iota(jnp.int32, (ROWS, LANES), 1)
    packed = jnp.zeros((ROWS, LANES), jnp.float32)
    for group in range(groups):
        wanted = jnp.sum(jnp.where(lane_active == row_active + group * ROWS, offsets, 0.0), 1, keepdims=True)
        chosen = lane_stars == wanted.astype(jnp.int32)
        for row in range(6):
            value = new_position[row:row + 1] if row < 3 else new_velocity[row - 3:row - 2]
            found = jnp.sum(jnp.where(chosen, value, 0.0), 1, keepdims=True)
            spread[0, group, row] = jnp.broadcast_to(found, (ROWS, LANES))
            packed = jnp.where(lane == group * ROWS + row, found, packed)
    targets[0] = packed

    pl.semaphore_wait(barrier, n_blk - 1 + n_grp - 1)
    near_last = sorted(range(1, n_blk), key=lambda k: -min(k, n_blk - k))
    target_copies = [None] + [
        pltpu.make_async_remote_copy(
            src_ref=targets.at[0], dst_ref=targets.at[back(k)],
            send_sem=tgt_send.at[k], recv_sem=tgt_recv.at[back(k)],
            device_id={"grp": mate(k)}, device_id_type=pl.DeviceIdType.MESH,
        )
        for k in range(1, n_grp)
    ]
    source_copies = [None] + [
        pltpu.make_async_remote_copy(
            src_ref=sources.at[0], dst_ref=sources.at[k],
            send_sem=src_send.at[k], recv_sem=src_recv.at[k],
            device_id={"blk": ahead(k)}, device_id_type=pl.DeviceIdType.MESH,
        )
        for k in range(1, n_blk)
    ]
    for k in near_last:
        source_copies[k].start()
    for k in range(n_grp - 1, 0, -1):
        target_copies[k].start()
    store_pred = pltpu.make_async_copy(out_pred, predicted, out_sem.at[0])
    store_pred.start()

    def pairs(slot, peer, totals):
        totals = list(totals)
        at = [[spread[peer, group, row] for row in range(6)] for group in range(groups)]
        for chunk in range(chunks):
            here = pl.ds(chunk * LANES, LANES)
            star = [jnp.broadcast_to(sources[slot, row:row + 1, here], (ROWS, LANES)) for row in range(7)]
            for group in range(groups):
                me = at[group]
                r = [star[d] - me[d] for d in range(3)]
                u = [star[3 + d] - me[3 + d] for d in range(3)]
                q = (r[0] * r[0] + r[1] * r[1] + r[2] * r[2]) + SOFTENING
                inverse = lax.rsqrt(q)
                square = inverse * inverse
                weight = star[6] * inverse * square
                radial = (r[0] * u[0] + r[1] * u[1] + r[2] * u[2]) * (3.0 * square)
                for d in range(3):
                    spot = group * 6 + d
                    totals[spot] = totals[spot] + weight * r[d]
                    totals[spot + 3] = totals[spot + 3] + weight * (u[d] - radial * r[d])
        return totals

    zeros = [jnp.zeros((ROWS, LANES), jnp.float32)] * (groups * 6)

    def keep(peer, totals):
        for at, value in enumerate(totals):
            sums[peer, at] = value

    def unpack(peer):
        block = targets[peer]
        for group in range(groups):
            for row in range(6):
                at = group * ROWS + row
                spread[peer, group, row] = jnp.broadcast_to(block[:, at:at + 1], (ROWS, LANES))

    order = [0] + near_last[::-1]
    last = order[-1]
    for place, slot in enumerate(order[:-1]):
        if slot:
            source_copies[slot].wait_recv()
        if place == 0:
            keep(0, pairs(slot, 0, zeros))
            for k in range(1, n_grp):
                target_copies[back(k)].wait_recv()

            @pl.loop(1, n_grp)
            def _(peer):
                unpack(peer)
                keep(peer, pairs(slot, peer, zeros))
        else:
            @pl.loop(0, n_grp)
            def _(peer):
                keep(peer, pairs(slot, peer, [sums[peer, at] for at in range(groups * 6)]))

    source_copies[last].wait_recv()
    sum_copies = {}
    for k in list(range(n_grp - 1, 0, -1)) + [0]:
        totals = pairs(last, k, [sums[k, at] for at in range(groups * 6)])
        packed = jnp.zeros((ROWS, LANES), jnp.float32)
        for group in range(groups):
            for row in range(6):
                value = jnp.sum(totals[group * 6 + row], 1, keepdims=True)
                packed = jnp.where(lane == group * ROWS + row, value, packed)
        if k:
            parts[k] = packed
            sum_copies[k] = pltpu.make_async_remote_copy(
                src_ref=parts.at[k], dst_ref=arrived.at[k],
                send_sem=sum_send.at[k], recv_sem=sum_recv.at[k],
                device_id={"grp": mate(k)}, device_id_type=pl.DeviceIdType.MESH,
            )
            sum_copies[k].start()
        else:
            total = packed
    for k in range(1, n_grp):
        sum_copies[k].wait_recv()
        total = total + arrived[k]
    turned = total.T
    for group in range(groups):
        here = pl.ds(group * ROWS, ROWS)
        out_acc[:, here] = turned[group * ROWS:group * ROWS + 3, :]
        out_jrk[:, here] = turned[group * ROWS + 3:group * ROWS + 6, :]
    store_acc = pltpu.make_async_copy(out_acc, accel, out_sem.at[1])
    store_jrk = pltpu.make_async_copy(out_jrk, jerk, out_sem.at[2])
    store_acc.start()
    store_jrk.start()
    for k in range(1, n_blk):
        source_copies[k].wait_send()
    for k in range(1, n_grp):
        target_copies[k].wait_send()
        sum_copies[k].wait_send()
    store_pred.wait()
    store_acc.wait()
    store_jrk.wait()


def local(n_blk, n_grp, position, velocity, accel_old, jerk_old, mass, elapsed, active_index):
    stars, active = position.shape[1], active_index.shape[0]
    groups = active // ROWS
    f32 = jnp.float32
    dma = pltpu.SemaphoreType.DMA
    any_spec = pl.BlockSpec(memory_space=pl.ANY)
    return pl.pallas_call(
        functools.partial(kernel, n_blk, n_grp, stars, active),
        out_shape=(
            jax.ShapeDtypeStruct((6, stars), f32),
            jax.ShapeDtypeStruct((3, active), f32),
            jax.ShapeDtypeStruct((3, active), f32),
        ),
        in_specs=[any_spec] * 7,
        out_specs=(any_spec,) * 3,
        scratch_shapes=[
            pltpu.VMEM((3, stars), f32), pltpu.VMEM((3, stars), f32),
            pltpu.VMEM((3, stars), f32), pltpu.VMEM((3, stars), f32),
            pltpu.VMEM((1, stars), f32), pltpu.VMEM((1, stars), f32),
            pltpu.VMEM((1, active), jnp.int32),
            pltpu.VMEM((6, stars), f32), pltpu.VMEM((3, active), f32), pltpu.VMEM((3, active), f32),
            pltpu.VMEM((n_blk, ROWS, stars), f32),
            pltpu.VMEM((n_grp, ROWS, LANES), f32),
            pltpu.VMEM((n_grp, groups, 6, ROWS, LANES), f32),
            pltpu.VMEM((n_grp, groups * 6, ROWS, LANES), f32),
            pltpu.VMEM((n_grp, ROWS, LANES), f32),
            pltpu.VMEM((n_grp, ROWS, LANES), f32),
            dma((7,)), dma((3,)), dma((n_blk,)), dma((n_blk,)),
            dma((n_grp,)), dma((n_grp,)), dma((n_grp,)), dma((n_grp,)),
        ],
        compiler_params=pltpu.CompilerParams(collective_id=0, has_side_effects=True),
        name="hermite",
    )(
        position, velocity, accel_old, jerk_old,
        mass.reshape(1, stars), elapsed.reshape(1, stars), active_index.reshape(1, active),
    )


def solution(mesh):
    split = P(None, ("blk", "grp"))
    single = P(("blk", "grp"))
    return jax.shard_map(
        functools.partial(local, mesh.shape["blk"], mesh.shape["grp"]),
        mesh=mesh,
        in_specs=(split, split, split, split, single, single, single),
        out_specs=(split, split, split),
        check_vma=False,
    )
```

```python
import functools

import jax
import jax.numpy as jnp
from jax import lax
from jax.experimental import pallas as pl
from jax.experimental.pallas import tpu as pltpu
from jax.sharding import PartitionSpec as P

SOFTENING = 0.0001
LANES = 128
ROWS = 8


def flipped(index, mask):
    out, bit = index, 1
    while bit <= mask:
        if mask & bit:
            out = out + bit - 2 * bit * lax.rem(lax.div(index, bit), 2)
        bit *= 2
    return out


def kernel(
    n_blk, n_grp, stars, active,
    position, velocity, accel_old, jerk_old, mass, elapsed, index,
    out_pred, out_sum,
    in_pos, in_vel, in_acc, in_jrk, in_mass, in_time, in_index,
    sources, targets, spread, sums, parts, arrived,
    in_sem, src_send, src_recv, tgt_send, tgt_recv, sum_send, sum_recv,
):
    blk, grp = lax.axis_index("blk"), lax.axis_index("grp")
    groups, chunks = active // ROWS, stars // LANES
    power_of_two = n_grp & (n_grp - 1) == 0

    def mate(k):
        return flipped(grp, k) if power_of_two else lax.rem(grp + k, n_grp)

    def back(k):
        return k if power_of_two else n_grp - k

    def ahead(k):
        return lax.rem(blk + k, n_blk)

    loads = [
        pltpu.make_async_copy(whole, held, in_sem.at[at])
        for at, (whole, held) in enumerate((
            (position, in_pos), (velocity, in_vel), (accel_old, in_acc), (jerk_old, in_jrk),
            (mass, in_mass), (elapsed, in_time), (index, in_index),
        ))
    ]
    for load in loads:
        load.start()

    barrier = pltpu.get_barrier_semaphore()
    for k in range(1, n_blk):
        pl.semaphore_signal(barrier, inc=1, device_id={"blk": ahead(k)}, device_id_type=pl.DeviceIdType.MESH)
    for k in range(1, n_grp):
        pl.semaphore_signal(barrier, inc=1, device_id={"grp": mate(k)}, device_id_type=pl.DeviceIdType.MESH)

    loads[-1].wait()
    base = (blk * n_grp + grp) * stars
    offsets = (in_index[...] - base).astype(jnp.float32)
    lane_active = lax.broadcasted_iota(jnp.int32, (ROWS, active), 1)
    row_active = lax.broadcasted_iota(jnp.int32, (ROWS, active), 0)
    wanted = [
        jnp.sum(jnp.where(lane_active == row_active + group * ROWS, offsets, 0.0), 1, keepdims=True)
        for group in range(groups)
    ]
    for load in loads[:-1]:
        load.wait()

    step_row = in_time[...]
    half = step_row * step_row * 0.5
    sixth = half * step_row * (1.0 / 3.0)
    new_position = in_pos[...] + step_row * in_vel[...] + half * in_acc[...] + sixth * in_jrk[...]
    new_velocity = in_vel[...] + step_row * in_acc[...] + half * in_jrk[...]
    sources[0, 0:3, :] = new_position
    sources[0, 3:6, :] = new_velocity
    sources[0, 6:7, :] = in_mass[...]
    out_pred[0:3, :] = new_position
    out_pred[3:6, :] = new_velocity

    pl.semaphore_wait(barrier, n_blk - 1 + n_grp - 1)
    near_last = sorted(range(1, n_blk), key=lambda k: -min(k, n_blk - k))
    target_copies = [None] + [
        pltpu.make_async_remote_copy(
            src_ref=targets.at[0], dst_ref=targets.at[back(k)],
            send_sem=tgt_send.at[k], recv_sem=tgt_recv.at[back(k)],
            device_id={"grp": mate(k)}, device_id_type=pl.DeviceIdType.MESH,
        )
        for k in range(1, n_grp)
    ]
    source_copies = [None] + [
        pltpu.make_async_remote_copy(
            src_ref=sources.at[0], dst_ref=sources.at[k],
            send_sem=src_send.at[k], recv_sem=src_recv.at[k],
            device_id={"blk": ahead(k)}, device_id_type=pl.DeviceIdType.MESH,
        )
        for k in range(1, n_blk)
    ]
    for k in near_last:
        source_copies[k].start()

    lane_stars = lax.broadcasted_iota(jnp.int32, (ROWS, stars), 1)
    lane = lax.broadcasted_iota(jnp.int32, (ROWS, LANES), 1)
    packed = jnp.zeros((ROWS, LANES), jnp.float32)
    for group in range(groups):
        chosen = lane_stars == wanted[group].astype(jnp.int32)
        for row in range(6):
            value = new_position[row:row + 1] if row < 3 else new_velocity[row - 3:row - 2]
            found = jnp.sum(jnp.where(chosen, value, 0.0), 1, keepdims=True)
            spread[0, group, row] = jnp.broadcast_to(found, (ROWS, LANES))
            packed = jnp.where(lane == group * ROWS + row, found, packed)
    targets[0] = packed
    for k in range(n_grp - 1, 0, -1):
        target_copies[k].start()

    def pairs(slot, peer, totals):
        totals = list(totals)
        at = [[spread[peer, group, row] for row in range(6)] for group in range(groups)]
        for chunk in range(chunks):
            here = pl.ds(chunk * LANES, LANES)
            star = [jnp.broadcast_to(sources[slot, row:row + 1, here], (ROWS, LANES)) for row in range(7)]
            for group in range(groups):
                me = at[group]
                r = [star[d] - me[d] for d in range(3)]
                u = [star[3 + d] - me[3 + d] for d in range(3)]
                q = (r[0] * r[0] + r[1] * r[1] + r[2] * r[2]) + SOFTENING
                inverse = lax.rsqrt(q)
                square = inverse * inverse
                weight = star[6] * inverse * square
                radial = (r[0] * u[0] + r[1] * u[1] + r[2] * u[2]) * (3.0 * square)
                for d in range(3):
                    spot = group * 6 + d
                    totals[spot] = totals[spot] + weight * r[d]
                    totals[spot + 3] = totals[spot + 3] + weight * (u[d] - radial * r[d])
        return totals

    zeros = [jnp.zeros((ROWS, LANES), jnp.float32)] * (groups * 6)

    def keep(peer, totals):
        for at, value in enumerate(totals):
            sums[peer, at] = value

    def unpack(peer):
        block = targets[peer]
        for group in range(groups):
            for row in range(6):
                at = group * ROWS + row
                spread[peer, group, row] = jnp.broadcast_to(block[:, at:at + 1], (ROWS, LANES))

    order = [0] + near_last[::-1]
    last = order[-1]
    for place, slot in enumerate(order[:-1]):
        if slot:
            source_copies[slot].wait_recv()
        if place == 0:
            keep(0, pairs(slot, 0, zeros))
            for k in range(1, n_grp):
                target_copies[back(k)].wait_recv()

            @pl.loop(1, n_grp)
            def _(peer):
                unpack(peer)
                keep(peer, pairs(slot, peer, zeros))
        else:
            @pl.loop(0, n_grp)
            def _(peer):
                keep(peer, pairs(slot, peer, [sums[peer, at] for at in range(groups * 6)]))

    source_copies[last].wait_recv()
    sum_copies = {}
    for k in list(range(n_grp - 1, 0, -1)) + [0]:
        totals = pairs(last, k, [sums[k, at] for at in range(groups * 6)])
        packed = jnp.zeros((ROWS, LANES), jnp.float32)
        for group in range(groups):
            for row in range(6):
                value = jnp.sum(totals[group * 6 + row], 1, keepdims=True)
                packed = jnp.where(lane == group * ROWS + row, value, packed)
        if k:
            parts[k] = packed
            sum_copies[k] = pltpu.make_async_remote_copy(
                src_ref=parts.at[k], dst_ref=arrived.at[k],
                send_sem=sum_send.at[k], recv_sem=sum_recv.at[k],
                device_id={"grp": mate(k)}, device_id_type=pl.DeviceIdType.MESH,
            )
            sum_copies[k].start()
        else:
            total = packed
    for k in range(1, n_grp):
        sum_copies[k].wait_recv()
        total = total + arrived[k]
    out_sum[...] = total
    for k in range(1, n_blk):
        source_copies[k].wait_send()
    for k in range(1, n_grp):
        target_copies[k].wait_send()
        sum_copies[k].wait_send()


def finish(groups, held, total, predicted, accel, jerk, out_acc, out_jrk, sem):
    store_pred = pltpu.make_async_copy(held, predicted, sem.at[0])
    store_pred.start()
    turned = total[...].T
    for group in range(groups):
        here = pl.ds(group * ROWS, ROWS)
        out_acc[:, here] = turned[group * ROWS:group * ROWS + 3, :]
        out_jrk[:, here] = turned[group * ROWS + 3:group * ROWS + 6, :]
    store_acc = pltpu.make_async_copy(out_acc, accel, sem.at[1])
    store_jrk = pltpu.make_async_copy(out_jrk, jerk, sem.at[2])
    store_acc.start()
    store_jrk.start()
    store_pred.wait()
    store_acc.wait()
    store_jrk.wait()


def local(n_blk, n_grp, position, velocity, accel_old, jerk_old, mass, elapsed, active_index):
    stars, active = position.shape[1], active_index.shape[0]
    groups = active // ROWS
    f32 = jnp.float32
    dma = pltpu.SemaphoreType.DMA
    hbm_spec = pl.BlockSpec(memory_space=pltpu.HBM)
    vmem_spec = pl.BlockSpec(memory_space=pltpu.VMEM)
    held, total = pl.pallas_call(
        functools.partial(kernel, n_blk, n_grp, stars, active),
        out_shape=(pltpu.VMEM((6, stars), f32), pltpu.VMEM((ROWS, LANES), f32)),
        in_specs=[hbm_spec] * 7,
        out_specs=(vmem_spec,) * 2,
        scratch_shapes=[
            pltpu.VMEM((3, stars), f32), pltpu.VMEM((3, stars), f32),
            pltpu.VMEM((3, stars), f32), pltpu.VMEM((3, stars), f32),
            pltpu.VMEM((1, stars), f32), pltpu.VMEM((1, stars), f32),
            pltpu.VMEM((1, active), jnp.int32),
            pltpu.VMEM((n_blk, ROWS, stars), f32),
            pltpu.VMEM((n_grp, ROWS, LANES), f32),
            pltpu.VMEM((n_grp, groups, 6, ROWS, LANES), f32),
            pltpu.VMEM((n_grp, groups * 6, ROWS, LANES), f32),
            pltpu.VMEM((n_grp, ROWS, LANES), f32),
            pltpu.VMEM((n_grp, ROWS, LANES), f32),
            dma((7,)), dma((n_blk,)), dma((n_blk,)),
            dma((n_grp,)), dma((n_grp,)), dma((n_grp,)), dma((n_grp,)),
        ],
        compiler_params=pltpu.CompilerParams(
            collective_id=0, has_side_effects=True,
        ),
        name="hermite",
    )(
        position, velocity, accel_old, jerk_old,
        mass.reshape(1, stars), elapsed.reshape(1, stars), active_index.reshape(1, active),
    )
    return pl.pallas_call(
        functools.partial(finish, groups),
        out_shape=(
            jax.ShapeDtypeStruct((6, stars), f32),
            jax.ShapeDtypeStruct((3, active), f32),
            jax.ShapeDtypeStruct((3, active), f32),
        ),
        in_specs=[vmem_spec] * 2,
        out_specs=(hbm_spec,) * 3,
        scratch_shapes=[pltpu.VMEM((3, active), f32), pltpu.VMEM((3, active), f32), dma((3,))],
        compiler_params=pltpu.CompilerParams(vmem_limit_bytes=16 * 1024 * 1024),
        name="finish",
    )(held, total)


def solution(mesh):
    split = P(None, ("blk", "grp"))
    single = P(("blk", "grp"))
    return jax.shard_map(
        functools.partial(local, mesh.shape["blk"], mesh.shape["grp"]),
        mesh=mesh,
        in_specs=(split, split, split, split, single, single, single),
        out_specs=(split, split, split),
        check_vma=False,
    )
```

```python
import functools

import jax
import jax.numpy as jnp
from jax import lax
from jax.experimental import pallas as pl
from jax.experimental.pallas import tpu as pltpu
from jax.sharding import PartitionSpec as P

SOFTENING = 0.0001
LANES = 128
ROWS = 8


def flipped(index, mask):
    out, bit = index, 1
    while bit <= mask:
        if mask & bit:
            out = out + bit - 2 * bit * lax.rem(lax.div(index, bit), 2)
        bit *= 2
    return out


def kernel(
    n_blk, n_grp, stars, active,
    position, velocity, accel_old, jerk_old, mass, elapsed, index,
    out_pred, out_sum,
    in_pos, in_vel, in_acc, in_jrk, in_mass, in_time, in_index,
    sources, targets, spread, sums, parts, arrived,
    in_sem, src_send, src_recv, tgt_send, tgt_recv, sum_send, sum_recv,
):
    blk, grp = lax.axis_index("blk"), lax.axis_index("grp")
    groups, chunks = active // ROWS, stars // LANES
    power_of_two = n_grp & (n_grp - 1) == 0

    def mate(k):
        return flipped(grp, k) if power_of_two else lax.rem(grp + k, n_grp)

    def back(k):
        return k if power_of_two else n_grp - k

    def ahead(k):
        return lax.rem(blk + k, n_blk)

    loads = [
        pltpu.make_async_copy(whole, held, in_sem.at[at])
        for at, (whole, held) in enumerate((
            (position, in_pos), (velocity, in_vel), (accel_old, in_acc), (jerk_old, in_jrk),
            (mass, in_mass), (elapsed, in_time), (index, in_index),
        ))
    ]
    for load in loads:
        load.start()

    barrier = pltpu.get_barrier_semaphore()
    for k in range(1, n_blk):
        pl.semaphore_signal(barrier, inc=1, device_id={"blk": ahead(k)}, device_id_type=pl.DeviceIdType.MESH)
    for k in range(1, n_grp):
        pl.semaphore_signal(barrier, inc=1, device_id={"grp": mate(k)}, device_id_type=pl.DeviceIdType.MESH)

    loads[-1].wait()
    base = (blk * n_grp + grp) * stars
    offsets = (in_index[...] - base).astype(jnp.float32)
    lane_active = lax.broadcasted_iota(jnp.int32, (ROWS, active), 1)
    row_active = lax.broadcasted_iota(jnp.int32, (ROWS, active), 0)
    wanted = [
        jnp.sum(jnp.where(lane_active == row_active + group * ROWS, offsets, 0.0), 1, keepdims=True)
        for group in range(groups)
    ]
    for load in loads[:-1]:
        load.wait()

    step_row = in_time[...]
    half = step_row * step_row * 0.5
    sixth = half * step_row * (1.0 / 3.0)
    new_position = in_pos[...] + step_row * in_vel[...] + half * in_acc[...] + sixth * in_jrk[...]
    new_velocity = in_vel[...] + step_row * in_acc[...] + half * in_jrk[...]
    sources[0, 0:3, :] = new_position
    sources[0, 3:6, :] = new_velocity
    sources[0, 6:7, :] = in_mass[...]
    out_pred[0:3, :] = new_position
    out_pred[3:6, :] = new_velocity

    pl.semaphore_wait(barrier, n_blk - 1 + n_grp - 1)
    order = [0] + sorted(range(1, n_blk), key=lambda k: min(k, n_blk - k))
    last = n_blk - 1
    target_copies = [None] + [
        pltpu.make_async_remote_copy(
            src_ref=targets.at[0], dst_ref=targets.at[back(k)],
            send_sem=tgt_send.at[k], recv_sem=tgt_recv.at[back(k)],
            device_id={"grp": mate(k)}, device_id_type=pl.DeviceIdType.MESH,
        )
        for k in range(1, n_grp)
    ]
    source_copies = [None] + [
        pltpu.make_async_remote_copy(
            src_ref=sources.at[0], dst_ref=sources.at[order.index(k)],
            send_sem=src_send.at[k], recv_sem=src_recv.at[k],
            device_id={"blk": ahead(k)}, device_id_type=pl.DeviceIdType.MESH,
        )
        for k in range(1, n_blk)
    ]
    for k in order[:0:-1]:
        source_copies[k].start()

    lane_stars = lax.broadcasted_iota(jnp.int32, (ROWS, stars), 1)
    lane = lax.broadcasted_iota(jnp.int32, (ROWS, LANES), 1)
    packed = jnp.zeros((ROWS, LANES), jnp.float32)
    for group in range(groups):
        chosen = lane_stars == wanted[group].astype(jnp.int32)
        for row in range(6):
            value = new_position[row:row + 1] if row < 3 else new_velocity[row - 3:row - 2]
            found = jnp.sum(jnp.where(chosen, value, 0.0), 1, keepdims=True)
            spread[0, group, row] = jnp.broadcast_to(found, (ROWS, LANES))
            packed = jnp.where(lane == group * ROWS + row, found, packed)
    targets[0] = packed
    for k in range(n_grp - 1, 0, -1):
        target_copies[k].start()

    def pairs(slot, peer, totals):
        totals = list(totals)
        at = [[spread[peer, group, row] for row in range(6)] for group in range(groups)]
        for chunk in range(chunks):
            here = pl.ds(chunk * LANES, LANES)
            star = [jnp.broadcast_to(sources[slot, row:row + 1, here], (ROWS, LANES)) for row in range(7)]
            for group in range(groups):
                me = at[group]
                r = [star[d] - me[d] for d in range(3)]
                u = [star[3 + d] - me[3 + d] for d in range(3)]
                q = (r[0] * r[0] + r[1] * r[1] + r[2] * r[2]) + SOFTENING
                inverse = lax.rsqrt(q)
                square = inverse * inverse
                weight = star[6] * inverse * square
                radial = (r[0] * u[0] + r[1] * u[1] + r[2] * u[2]) * (3.0 * square)
                for d in range(3):
                    spot = group * 6 + d
                    totals[spot] = totals[spot] + weight * r[d]
                    totals[spot + 3] = totals[spot + 3] + weight * (u[d] - radial * r[d])
        return totals

    zeros = (jnp.zeros((ROWS, LANES), jnp.float32),) * (groups * 6)

    def over(first, end, peer, totals):
        return lax.fori_loop(first, end, lambda place, held: tuple(pairs(place, peer, held)), tuple(totals))

    def keep(peer, totals):
        for at, value in enumerate(totals):
            sums[peer, at] = value

    def kept(peer):
        return tuple(sums[peer, at] for at in range(groups * 6))

    def unpack(peer):
        target_copies[back(peer)].wait_recv()
        block = targets[peer]
        for group in range(groups):
            for row in range(6):
                at = group * ROWS + row
                spread[peer, group, row] = jnp.broadcast_to(block[:, at:at + 1], (ROWS, LANES))

    def pack(totals):
        packed = jnp.zeros((ROWS, LANES), jnp.float32)
        for group in range(groups):
            for row in range(6):
                value = jnp.sum(totals[group * 6 + row], 1, keepdims=True)
                packed = jnp.where(lane == group * ROWS + row, value, packed)
        return packed

    sum_copies = {}

    def send(k, totals):
        parts[k] = pack(totals)
        sum_copies[k] = pltpu.make_async_remote_copy(
            src_ref=parts.at[k], dst_ref=arrived.at[k],
            send_sem=sum_send.at[k], recv_sem=sum_recv.at[k],
            device_id={"grp": mate(k)}, device_id_type=pl.DeviceIdType.MESH,
        )
        sum_copies[k].start()

    far = list(range(n_grp - 1, 0, -1))
    lead = max(1, n_grp // 4)
    totals = over(0, 1, 0, zeros)
    for k in order[1:-1]:
        source_copies[k].wait_recv()
    keep(0, over(1, last, 0, totals))
    for k in far[:lead]:
        unpack(k)
        keep(k, over(0, last, k, zeros))
    if last:
        source_copies[order[last]].wait_recv()
    for k in far[:lead]:
        send(k, over(last, n_blk, k, kept(k)))
    for k in far[lead:]:
        unpack(k)
        send(k, over(0, n_blk, k, zeros))
    total = pack(over(last, n_blk, 0, kept(0)))
    for k in range(1, n_grp):
        sum_copies[k].wait_recv()
        total = total + arrived[k]
    out_sum[...] = total
    for k in range(1, n_blk):
        source_copies[k].wait_send()
    for k in range(1, n_grp):
        target_copies[k].wait_send()
        sum_copies[k].wait_send()


def finish(groups, held, total, predicted, accel, jerk, out_acc, out_jrk, sem):
    store_pred = pltpu.make_async_copy(held, predicted, sem.at[0])
    store_pred.start()
    turned = total[...].T
    for group in range(groups):
        here = pl.ds(group * ROWS, ROWS)
        out_acc[:, here] = turned[group * ROWS:group * ROWS + 3, :]
        out_jrk[:, here] = turned[group * ROWS + 3:group * ROWS + 6, :]
    store_acc = pltpu.make_async_copy(out_acc, accel, sem.at[1])
    store_jrk = pltpu.make_async_copy(out_jrk, jerk, sem.at[2])
    store_acc.start()
    store_jrk.start()
    store_pred.wait()
    store_acc.wait()
    store_jrk.wait()


def local(n_blk, n_grp, position, velocity, accel_old, jerk_old, mass, elapsed, active_index):
    stars, active = position.shape[1], active_index.shape[0]
    groups = active // ROWS
    f32 = jnp.float32
    dma = pltpu.SemaphoreType.DMA
    hbm_spec = pl.BlockSpec(memory_space=pltpu.HBM)
    vmem_spec = pl.BlockSpec(memory_space=pltpu.VMEM)
    held, total = pl.pallas_call(
        functools.partial(kernel, n_blk, n_grp, stars, active),
        out_shape=(pltpu.VMEM((6, stars), f32), pltpu.VMEM((ROWS, LANES), f32)),
        in_specs=[hbm_spec] * 7,
        out_specs=(vmem_spec,) * 2,
        scratch_shapes=[
            pltpu.VMEM((3, stars), f32), pltpu.VMEM((3, stars), f32),
            pltpu.VMEM((3, stars), f32), pltpu.VMEM((3, stars), f32),
            pltpu.VMEM((1, stars), f32), pltpu.VMEM((1, stars), f32),
            pltpu.VMEM((1, active), jnp.int32),
            pltpu.VMEM((n_blk, ROWS, stars), f32),
            pltpu.VMEM((n_grp, ROWS, LANES), f32),
            pltpu.VMEM((n_grp, groups, 6, ROWS, LANES), f32),
            pltpu.VMEM((n_grp, groups * 6, ROWS, LANES), f32),
            pltpu.VMEM((n_grp, ROWS, LANES), f32),
            pltpu.VMEM((n_grp, ROWS, LANES), f32),
            dma((7,)), dma((n_blk,)), dma((n_blk,)),
            dma((n_grp,)), dma((n_grp,)), dma((n_grp,)), dma((n_grp,)),
        ],
        compiler_params=pltpu.CompilerParams(
            collective_id=0, has_side_effects=True,
        ),
        name="hermite",
    )(
        position, velocity, accel_old, jerk_old,
        mass.reshape(1, stars), elapsed.reshape(1, stars), active_index.reshape(1, active),
    )
    return pl.pallas_call(
        functools.partial(finish, groups),
        out_shape=(
            jax.ShapeDtypeStruct((6, stars), f32),
            jax.ShapeDtypeStruct((3, active), f32),
            jax.ShapeDtypeStruct((3, active), f32),
        ),
        in_specs=[vmem_spec] * 2,
        out_specs=(hbm_spec,) * 3,
        scratch_shapes=[pltpu.VMEM((3, active), f32), pltpu.VMEM((3, active), f32), dma((3,))],
        compiler_params=pltpu.CompilerParams(vmem_limit_bytes=16 * 1024 * 1024),
        name="finish",
    )(held, total)


def solution(mesh):
    split = P(None, ("blk", "grp"))
    single = P(("blk", "grp"))
    return jax.shard_map(
        functools.partial(local, mesh.shape["blk"], mesh.shape["grp"]),
        mesh=mesh,
        in_specs=(split, split, split, split, single, single, single),
        out_specs=(split, split, split),
        check_vma=False,
    )
```

```python
import functools

import jax
import jax.numpy as jnp
from jax import lax
from jax.experimental import pallas as pl
from jax.experimental.pallas import tpu as pltpu
from jax.sharding import PartitionSpec as P

SOFTENING = 0.0001
LANES = 128
ROWS = 8


def flipped(index, mask):
    out, bit = index, 1
    while bit <= mask:
        if mask & bit:
            out = out + bit - 2 * bit * lax.rem(lax.div(index, bit), 2)
        bit *= 2
    return out


def kernel(
    n_blk, n_grp, stars, active,
    position, velocity, accel_old, jerk_old, mass, elapsed, index,
    out_pred, out_sum,
    in_pos, in_vel, in_acc, in_jrk, in_mass, in_time, in_index,
    sources, targets, spread, sums, parts, arrived,
    in_sem, src_send, src_recv, tgt_send, tgt_recv, sum_send, sum_recv,
):
    blk, grp = lax.axis_index("blk"), lax.axis_index("grp")
    groups, chunks = active // ROWS, stars // LANES
    power_of_two = n_grp & (n_grp - 1) == 0

    def mate(k):
        return flipped(grp, k) if power_of_two else lax.rem(grp + k, n_grp)

    def back(k):
        return k if power_of_two else n_grp - k

    def ahead(k):
        return lax.rem(blk + k, n_blk)

    loads = [
        pltpu.make_async_copy(whole, held, in_sem.at[at])
        for at, (whole, held) in enumerate((
            (position, in_pos), (velocity, in_vel), (accel_old, in_acc), (jerk_old, in_jrk),
            (mass, in_mass), (elapsed, in_time), (index, in_index),
        ))
    ]
    for load in loads:
        load.start()

    barrier = pltpu.get_barrier_semaphore()
    for k in range(1, n_blk):
        pl.semaphore_signal(barrier, inc=1, device_id={"blk": ahead(k)}, device_id_type=pl.DeviceIdType.MESH)
    for k in range(1, n_grp):
        pl.semaphore_signal(barrier, inc=1, device_id={"grp": mate(k)}, device_id_type=pl.DeviceIdType.MESH)

    loads[-1].wait()
    base = (blk * n_grp + grp) * stars
    offsets = (in_index[...] - base).astype(jnp.float32)
    lane_active = lax.broadcasted_iota(jnp.int32, (ROWS, active), 1)
    row_active = lax.broadcasted_iota(jnp.int32, (ROWS, active), 0)
    wanted = [
        jnp.sum(jnp.where(lane_active == row_active + group * ROWS, offsets, 0.0), 1, keepdims=True)
        for group in range(groups)
    ]
    for load in loads[:-1]:
        load.wait()

    step_row = in_time[...]
    half = step_row * step_row * 0.5
    sixth = half * step_row * (1.0 / 3.0)
    new_position = in_pos[...] + step_row * in_vel[...] + half * in_acc[...] + sixth * in_jrk[...]
    new_velocity = in_vel[...] + step_row * in_acc[...] + half * in_jrk[...]
    sources[0, 0:3, :] = new_position
    sources[0, 3:6, :] = new_velocity
    sources[0, 6:7, :] = in_mass[...]
    out_pred[0:3, :] = new_position
    out_pred[3:6, :] = new_velocity

    pl.semaphore_wait(barrier, n_blk - 1 + n_grp - 1)
    order = [0] + sorted(range(1, n_blk), key=lambda k: min(k, n_blk - k))
    last = n_blk - 1
    target_copies = [None] + [
        pltpu.make_async_remote_copy(
            src_ref=targets.at[0], dst_ref=targets.at[back(k)],
            send_sem=tgt_send.at[k], recv_sem=tgt_recv.at[back(k)],
            device_id={"grp": mate(k)}, device_id_type=pl.DeviceIdType.MESH,
        )
        for k in range(1, n_grp)
    ]
    source_copies = [None] + [
        pltpu.make_async_remote_copy(
            src_ref=sources.at[0], dst_ref=sources.at[order.index(k)],
            send_sem=src_send.at[k], recv_sem=src_recv.at[k],
            device_id={"blk": ahead(k)}, device_id_type=pl.DeviceIdType.MESH,
        )
        for k in range(1, n_blk)
    ]
    for k in order[:0:-1]:
        source_copies[k].start()

    lane_stars = lax.broadcasted_iota(jnp.int32, (ROWS, stars), 1)
    lane = lax.broadcasted_iota(jnp.int32, (ROWS, LANES), 1)
    packed = jnp.zeros((ROWS, LANES), jnp.float32)
    for group in range(groups):
        chosen = lane_stars == wanted[group].astype(jnp.int32)
        for row in range(6):
            value = new_position[row:row + 1] if row < 3 else new_velocity[row - 3:row - 2]
            found = jnp.sum(jnp.where(chosen, value, 0.0), 1, keepdims=True)
            spread[0, group, row] = jnp.broadcast_to(found, (ROWS, LANES))
            packed = jnp.where(lane == group * ROWS + row, found, packed)
    targets[0] = packed
    for k in range(n_grp - 1, 0, -1):
        target_copies[k].start()

    def pairs(slot, peer, totals):
        totals = list(totals)
        at = [[spread[peer, group, row] for row in range(6)] for group in range(groups)]
        for chunk in range(chunks):
            here = pl.ds(chunk * LANES, LANES)
            star = [jnp.broadcast_to(sources[slot, row:row + 1, here], (ROWS, LANES)) for row in range(7)]
            for group in range(groups):
                me = at[group]
                r = [star[d] - me[d] for d in range(3)]
                u = [star[3 + d] - me[3 + d] for d in range(3)]
                q = (r[0] * r[0] + r[1] * r[1] + r[2] * r[2]) + SOFTENING
                inverse = lax.rsqrt(q)
                square = inverse * inverse
                weight = star[6] * inverse * square
                radial = (r[0] * u[0] + r[1] * u[1] + r[2] * u[2]) * (3.0 * square)
                for d in range(3):
                    spot = group * 6 + d
                    totals[spot] = totals[spot] + weight * r[d]
                    totals[spot + 3] = totals[spot + 3] + weight * (u[d] - radial * r[d])
        return totals

    zeros = (jnp.zeros((ROWS, LANES), jnp.float32),) * (groups * 6)

    def over(first, end, peer, totals):
        return lax.fori_loop(first, end, lambda place, held: tuple(pairs(place, peer, held)), tuple(totals), unroll=end - first <= 4)

    def keep(peer, totals):
        for at, value in enumerate(totals):
            sums[peer, at] = value

    def kept(peer):
        return tuple(sums[peer, at] for at in range(groups * 6))

    def unpack(peer):
        target_copies[back(peer)].wait_recv()
        block = targets[peer]
        for group in range(groups):
            for row in range(6):
                at = group * ROWS + row
                spread[peer, group, row] = jnp.broadcast_to(block[:, at:at + 1], (ROWS, LANES))

    def pack(totals):
        packed = jnp.zeros((ROWS, LANES), jnp.float32)
        for group in range(groups):
            for row in range(6):
                value = jnp.sum(totals[group * 6 + row], 1, keepdims=True)
                packed = jnp.where(lane == group * ROWS + row, value, packed)
        return packed

    sum_copies = {}

    def send(k, totals):
        parts[k] = pack(totals)
        sum_copies[k] = pltpu.make_async_remote_copy(
            src_ref=parts.at[k], dst_ref=arrived.at[k],
            send_sem=sum_send.at[k], recv_sem=sum_recv.at[k],
            device_id={"grp": mate(k)}, device_id_type=pl.DeviceIdType.MESH,
        )
        sum_copies[k].start()

    far = list(range(n_grp - 1, 0, -1))
    keep(0, over(0, 1, 0, zeros))
    for k in far:
        unpack(k)
        keep(k, over(0, 1, k, zeros))
    for k in order[1:]:
        source_copies[k].wait_recv()
    for k in far:
        send(k, over(1, n_blk, k, kept(k)))
    total = pack(over(1, n_blk, 0, kept(0)))
    for k in range(1, n_grp):
        sum_copies[k].wait_recv()
        total = total + arrived[k]
    out_sum[...] = total
    for k in range(1, n_blk):
        source_copies[k].wait_send()
    for k in range(1, n_grp):
        target_copies[k].wait_send()
        sum_copies[k].wait_send()


def finish(groups, held, total, predicted, accel, jerk, out_acc, out_jrk, sem):
    store_pred = pltpu.make_async_copy(held, predicted, sem.at[0])
    store_pred.start()
    turned = total[...].T
    for group in range(groups):
        here = pl.ds(group * ROWS, ROWS)
        out_acc[:, here] = turned[group * ROWS:group * ROWS + 3, :]
        out_jrk[:, here] = turned[group * ROWS + 3:group * ROWS + 6, :]
    store_acc = pltpu.make_async_copy(out_acc, accel, sem.at[1])
    store_jrk = pltpu.make_async_copy(out_jrk, jerk, sem.at[2])
    store_acc.start()
    store_jrk.start()
    store_pred.wait()
    store_acc.wait()
    store_jrk.wait()


def local(n_blk, n_grp, position, velocity, accel_old, jerk_old, mass, elapsed, active_index):
    stars, active = position.shape[1], active_index.shape[0]
    groups = active // ROWS
    f32 = jnp.float32
    dma = pltpu.SemaphoreType.DMA
    hbm_spec = pl.BlockSpec(memory_space=pltpu.HBM)
    vmem_spec = pl.BlockSpec(memory_space=pltpu.VMEM)
    held, total = pl.pallas_call(
        functools.partial(kernel, n_blk, n_grp, stars, active),
        out_shape=(pltpu.VMEM((6, stars), f32), pltpu.VMEM((ROWS, LANES), f32)),
        in_specs=[hbm_spec] * 7,
        out_specs=(vmem_spec,) * 2,
        scratch_shapes=[
            pltpu.VMEM((3, stars), f32), pltpu.VMEM((3, stars), f32),
            pltpu.VMEM((3, stars), f32), pltpu.VMEM((3, stars), f32),
            pltpu.VMEM((1, stars), f32), pltpu.VMEM((1, stars), f32),
            pltpu.VMEM((1, active), jnp.int32),
            pltpu.VMEM((n_blk, ROWS, stars), f32),
            pltpu.VMEM((n_grp, ROWS, LANES), f32),
            pltpu.VMEM((n_grp, groups, 6, ROWS, LANES), f32),
            pltpu.VMEM((n_grp, groups * 6, ROWS, LANES), f32),
            pltpu.VMEM((n_grp, ROWS, LANES), f32),
            pltpu.VMEM((n_grp, ROWS, LANES), f32),
            dma((7,)), dma((n_blk,)), dma((n_blk,)),
            dma((n_grp,)), dma((n_grp,)), dma((n_grp,)), dma((n_grp,)),
        ],
        compiler_params=pltpu.CompilerParams(
            collective_id=0, has_side_effects=True,
        ),
        name="hermite",
    )(
        position, velocity, accel_old, jerk_old,
        mass.reshape(1, stars), elapsed.reshape(1, stars), active_index.reshape(1, active),
    )
    return pl.pallas_call(
        functools.partial(finish, groups),
        out_shape=(
            jax.ShapeDtypeStruct((6, stars), f32),
            jax.ShapeDtypeStruct((3, active), f32),
            jax.ShapeDtypeStruct((3, active), f32),
        ),
        in_specs=[vmem_spec] * 2,
        out_specs=(hbm_spec,) * 3,
        scratch_shapes=[pltpu.VMEM((3, active), f32), pltpu.VMEM((3, active), f32), dma((3,))],
        compiler_params=pltpu.CompilerParams(vmem_limit_bytes=16 * 1024 * 1024),
        name="finish",
    )(held, total)


def solution(mesh):
    split = P(None, ("blk", "grp"))
    single = P(("blk", "grp"))
    return jax.shard_map(
        functools.partial(local, mesh.shape["blk"], mesh.shape["grp"]),
        mesh=mesh,
        in_specs=(split, split, split, split, single, single, single),
        out_specs=(split, split, split),
        check_vma=False,
    )
```
